32 devices in a mesh: group: 16 (over z, x, core), tensor: 2 (over y).
Axes of the slice: x: 2, y: 2, z: 4, core: 2. Of those that a mesh axis runs over, the one named last changes fastest.
Arguments:
- prompt_cache: bfloat16 [2, 65536, 1024], P(None, ('group', 'tensor')), may hold values from -6 to 6
- queries: bfloat16 [32, 64, 8192], P('group', None, 'tensor'), may hold values from -10 to 10
- new_cache: bfloat16 [2, 32, 64, 1024], P(None, 'group', None, 'tensor'), may hold values from -6 to 6
- offsets: int32 [16, 2], P('group'), may hold values from 0 to 3
- lengths: int32 [16], P('group'), may hold values from 64 to 4096
- block_table: int32 [16, 32], P('group'), may hold values from 0 to 31, each once within a row
Outputs:
- attention: bfloat16 [32, 64, 8192], P('group', None, 'tensor')
The draws below stay inside these ranges and needn't reach their ends.
Inputs may be any that keep to these rules, and one draw needn't show every extreme that they name: Each row of block_table names each of the 32 stored blocks of its prompt once.
All inputs are finite; a program needn't handle non-finite values.
Results may differ from the reference program's by a relative error of at most 0.0095.
Values may be sent and summed in bfloat16 or wider, within the bound.
A program may use at most 128 MiB of HBM per device.

```python
import jax
import jax.numpy as jnp
from jax import lax

QH = 64
KVH = 8
HD = 128
BLOCK = 128
MAXB = 32
SAMPLES = 16
STEPS = 4
REACH = 4
CAP = 2
N_GROUP = 16


def base_queries(key):
    array_shape = (N_GROUP * CAP, SAMPLES * STEPS, QH * HD)
    drawn = jax.random.normal(jax.random.fold_in(key, 2101), array_shape, jnp.float32)
    return jnp.clip(drawn, -6.0, 6.0)


def draw_queries(key, part):
    drawn = base_queries(key)
    return drawn.astype(jnp.bfloat16)


def draw_prompt_cache(key, part):
    tokens = N_GROUP * MAXB * BLOCK
    array_shape = (2, tokens, KVH * HD)
    drawn = jnp.clip(jax.random.normal(jax.random.fold_in(key, 1101), array_shape, jnp.float32), -6.0, 6.0)
    return drawn.astype(jnp.bfloat16)


def draw_new_cache(key, part):
    array_shape = (N_GROUP * CAP, SAMPLES * STEPS, KVH * HD)
    grouped = base_queries(key).reshape(N_GROUP * CAP, SAMPLES * STEPS, KVH, QH // KVH, HD)
    grouped = jnp.mean(grouped, axis=3).reshape(array_shape)
    noise = jax.random.normal(jax.random.fold_in(key, 3101), array_shape, jnp.float32)
    key_part = jnp.clip(3.5 * grouped + 0.5 * noise, -6.0, 6.0)
    values = jnp.clip(jax.random.normal(jax.random.fold_in(key, 3102), array_shape, jnp.float32), -6.0, 6.0)
    return jnp.stack([key_part, values]).astype(jnp.bfloat16)


def place_ends(result, own_key, smallest, top_value):
    dims = result.shape
    place = [jax.random.randint(jax.random.fold_in(own_key, axis), (), 0, dims[axis]) for axis in range(len(dims))]
    result = result.at[tuple(place)].set(smallest)
    longest = dims.index(max(dims))
    place[longest] = (place[longest] + 1) % dims[longest]
    return result.at[tuple(place)].set(top_value)


def setup_inputs(seed: int = 0) -> dict:
    splits = jax.random.split(jax.random.key(seed), 7)
    prompt_cache = draw_prompt_cache(jax.random.fold_in(splits[6], 71), 0)
    queries = draw_queries(jax.random.fold_in(splits[6], 71), 0)
    new_cache = draw_new_cache(jax.random.fold_in(splits[6], 71), 0)
    offsets = place_ends(jax.random.randint(splits[3], (N_GROUP, CAP), 0, REACH), jax.random.fold_in(splits[3], 1), 0, REACH - 1).astype(jnp.int32)
    lengths = place_ends(jax.random.randint(splits[4], (N_GROUP,), BLOCK // 2, MAXB * BLOCK + 1), jax.random.fold_in(splits[4], 1), BLOCK // 2, MAXB * BLOCK).astype(jnp.int32)
    block_table = jax.vmap(lambda own: jax.random.permutation(own, MAXB))(jax.random.split(splits[5], N_GROUP)).reshape((N_GROUP, MAXB)).astype(jnp.int32)
    return {"prompt_cache": prompt_cache, "queries": queries, "new_cache": new_cache, "offsets": offsets, "lengths": lengths, "block_table": block_table}


masked_score = -1e30


def live_tokens(table_row, length, block_size):
    blocks = table_row.shape[0]
    physical = jnp.arange(blocks, dtype=jnp.int32)
    logical = jnp.sum(physical[:, None] * (table_row[:, None] == physical[None, :]).astype(jnp.int32), axis=0)
    position = logical[:, None] * block_size + jnp.arange(block_size, dtype=jnp.int32)[None, :]
    return position.reshape(-1) < length


def prompt_block(query_rows, prompt_keys, prompt_values, live_mask):
    row_count = query_rows.shape[0]
    kv_heads = prompt_keys.shape[1] // HD
    group_size = query_rows.shape[1] // (kv_heads * HD)
    query_split = query_rows.astype(jnp.float32).reshape(row_count, kv_heads, group_size, HD)
    key_split = prompt_keys.astype(jnp.float32).reshape(-1, kv_heads, HD)
    value_split = prompt_values.astype(jnp.float32).reshape(-1, kv_heads, HD)
    scores = jnp.einsum("rgkd,pgd->gkrp", query_split, key_split, precision=lax.Precision.HIGHEST) * (HD ** -0.5)
    scores = jnp.where(live_mask[None, None, None, :], scores, masked_score)
    prompt_peak = jnp.max(scores, axis=-1)
    weights = jnp.exp(scores - prompt_peak[..., None])
    prompt_total = jnp.sum(weights, axis=-1)
    rounded = lax.optimization_barrier(weights.astype(jnp.bfloat16)).astype(jnp.float32)
    numerator = jnp.einsum("gkrp,pgd->rgkd", rounded, value_split, precision=lax.Precision.HIGHEST)
    total_rows = jnp.transpose(prompt_total, (2, 0, 1))
    prompt_part = (numerator / total_rows[..., None]).astype(jnp.bfloat16)
    return prompt_part, jnp.transpose(prompt_peak, (2, 0, 1)), total_rows


def own_block(query_rows, new_keys, new_values):
    kv_heads = new_keys.shape[1] // HD
    group_size = query_rows.shape[1] // (kv_heads * HD)
    row_count = SAMPLES * STEPS
    query_split = query_rows.astype(jnp.float32).reshape(SAMPLES, STEPS, kv_heads, group_size, HD)
    key_split = new_keys.astype(jnp.float32).reshape(SAMPLES, STEPS, kv_heads, HD)
    value_split = new_values.astype(jnp.float32).reshape(SAMPLES, STEPS, kv_heads, HD)
    scores = jnp.einsum("stgkd,sugd->stgku", query_split, key_split, precision=lax.Precision.HIGHEST) * (HD ** -0.5)
    steps_index = jnp.arange(STEPS, dtype=jnp.int32)
    causal = (steps_index[:, None] >= steps_index[None, :])[None, :, None, None, :]
    scores = jnp.where(causal, scores, masked_score)
    own_peak = jnp.max(scores, axis=-1)
    weights = jnp.exp(scores - own_peak[..., None])
    own_total = jnp.sum(weights, axis=-1)
    rounded = lax.optimization_barrier(weights.astype(jnp.bfloat16)).astype(jnp.float32)
    own_sum = jnp.einsum("stgku,sugd->stgkd", rounded, value_split, precision=lax.Precision.HIGHEST)
    return (own_sum.reshape(row_count, kv_heads, group_size, HD),
            own_peak.reshape(row_count, kv_heads, group_size),
            own_total.reshape(row_count, kv_heads, group_size))


def merge_parts(prompt_stats, own_stats):
    prompt_part, prompt_peak, prompt_total = prompt_stats
    own_sum, own_peak, own_total = own_stats
    prompt_part = lax.optimization_barrier(prompt_part)
    highest = jnp.maximum(prompt_peak, own_peak)
    prompt_scale = prompt_total * jnp.exp(prompt_peak - highest)
    own_scale = jnp.exp(own_peak - highest)
    numerator_all = prompt_scale[..., None] * prompt_part.astype(jnp.float32) + own_scale[..., None] * own_sum
    denominator = prompt_scale + own_total * own_scale
    merged = numerator_all / denominator[..., None]
    return merged.reshape(merged.shape[0], -1).astype(jnp.bfloat16)


def reference(prompt_cache, queries, new_cache, offsets, lengths, block_table):
    prompt_tokens = MAXB * BLOCK
    all_keys = prompt_cache[0]
    all_values = prompt_cache[1]
    new_keys_all = new_cache[0]
    new_values_all = new_cache[1]
    flat_offsets = offsets.reshape(-1)

    def serve_slot(slot):
        decode_group = slot // CAP
        distance = flat_offsets[slot]
        prompt = ((decode_group - distance) % N_GROUP).astype(jnp.int32)
        start = (prompt * prompt_tokens).astype(jnp.int32)
        prompt_keys = lax.dynamic_slice_in_dim(all_keys, start, prompt_tokens, 0)
        prompt_values = lax.dynamic_slice_in_dim(all_values, start, prompt_tokens, 0)
        live_mask = live_tokens(block_table[prompt], lengths[prompt], BLOCK)
        query_rows = lax.dynamic_index_in_dim(queries, slot, 0, keepdims=False)
        new_keys = lax.dynamic_index_in_dim(new_keys_all, slot, 0, keepdims=False)
        new_values = lax.dynamic_index_in_dim(new_values_all, slot, 0, keepdims=False)
        prompt_stats = prompt_block(query_rows, prompt_keys, prompt_values, live_mask)
        own_stats = own_block(query_rows, new_keys, new_values)
        return merge_parts(prompt_stats, own_stats)

    indices = jnp.arange(N_GROUP * CAP, dtype=jnp.int32)
    return lax.map(serve_slot, indices)
```

```python
from functools import partial

import jax
import jax.numpy as jnp
from jax import lax
from jax.experimental import pallas as pl
from jax.experimental.pallas import tpu as pltpu
from jax.sharding import PartitionSpec as P

HD = 128
BLOCK = 128
STEPS = 4
REACH = 4
TEAM = 2
GATHER = 4
LOG2E = 1.4426950408889634
LN2 = 0.6931471805599453
AXES = ("group", "tensor")

masked_score = -1e30


def prompt_kernel(sub, members, links, cap, group_size, info_ref, *refs):
    count = len(links)
    kv_refs = refs[: sub * members]
    query_refs = refs[sub * members : sub * members + count]
    out_refs = refs[sub * members + count : sub * members + 2 * count]
    keys, values, sems = refs[sub * members + 2 * count :]
    tokens = kv_refs[0].shape[1]
    rows = query_refs[0].shape[1]
    wide = rows * group_size
    chunk = GATHER * BLOCK
    factor = HD ** -0.5 * LOG2E

    copies = []
    for j in range(sub):
        for r in range(members):
            source = kv_refs[j * members + r]
            for part, target in ((0, keys), (1, values)):
                copy = pltpu.make_async_copy(
                    source.at[part],
                    target.at[j, pl.ds(r * tokens, tokens), :],
                    sems.at[j, r, part],
                )
                copy.start()
                copies.append(copy)
    for copy in copies:
        copy.wait()

    lane = lax.broadcasted_iota(jnp.int32, (rows, HD), 1)
    token_row = lax.broadcasted_iota(jnp.int32, (chunk, wide), 0)
    blocks = members * tokens // BLOCK

    for n in range(count):
        query_ref = query_refs[n]
        out_ref = out_refs[n]

        def one(c, carry, n=n, query_ref=query_ref, out_ref=out_ref):
            j = info_ref[sub * (blocks + 1) + n * cap + c]

            @pl.when(j >= 0)
            def _():
                base = j * (blocks + 1)
                length = info_ref[base]
                query = jnp.concatenate(
                    [query_ref[c, :, g * HD : (g + 1) * HD] for g in range(group_size)], axis=0
                )

                def step(masked, i, state):
                    peak, total, acc = state
                    key_parts, value_parts = [], []
                    for u in range(GATHER):
                        where = info_ref[base + 1 + i * GATHER + u]
                        rows_at = pl.ds(pl.multiple_of(where * BLOCK, BLOCK), BLOCK)
                        key_parts.append(keys[j, rows_at, :])
                        value_parts.append(values[j, rows_at, :])
                    key = jnp.concatenate(key_parts, axis=0)
                    value = jnp.concatenate(value_parts, axis=0)
                    scores = lax.dot_general(
                        key, query, (((1,), (1,)), ((), ())), preferred_element_type=jnp.float32
                    )
                    if masked:
                        scores = jnp.where(token_row < length - i * chunk, scores, masked_score)
                    new_peak = jnp.maximum(peak, jnp.max(scores, axis=0, keepdims=True))
                    shift = new_peak * factor
                    weights = jnp.exp2(scores * factor - shift)
                    decay = jnp.exp2(peak * factor - shift)
                    total = total * decay + jnp.sum(weights, axis=0, keepdims=True)
                    acc = acc * decay + lax.dot_general(
                        value,
                        weights.astype(jnp.bfloat16),
                        (((0,), (0,)), ((), ())),
                        preferred_element_type=jnp.float32,
                    )
                    return new_peak, total, acc

                state = (
                    jnp.full((1, wide), masked_score, jnp.float32),
                    jnp.zeros((1, wide), jnp.float32),
                    jnp.zeros((HD, wide), jnp.float32),
                )
                full = length // chunk
                state = lax.fori_loop(0, full, partial(step, False), state)
                state = lax.fori_loop(full, (length + chunk - 1) // chunk, partial(step, True), state)
                peak, total, acc = state
                result = jnp.transpose(acc / total)
                level = peak * HD ** -0.5 + jnp.log(total)
                level = jnp.transpose(jnp.broadcast_to(level, (HD, wide)))
                stats = jnp.zeros((rows, HD), jnp.float32)
                for g in range(group_size):
                    span = slice(g * rows, (g + 1) * rows)
                    out_ref[c, :, g * HD : (g + 1) * HD] = result[span].astype(jnp.bfloat16)
                    high = level[span].astype(jnp.bfloat16).astype(jnp.float32)
                    low = level[span] - high
                    stats = jnp.where(lane == g, high, stats)
                    stats = jnp.where(lane == group_size + g, low, stats)
                out_ref[c, :, group_size * HD :] = stats.astype(jnp.bfloat16)

            return carry

        lax.fori_loop(0, cap, one, 0)


def prompt_call(sub, members, links, cap, group_size, stage, info, chunks, fetched):
    rows = fetched[0].shape[1]
    tokens = chunks[0].shape[1]
    width = group_size * HD
    count = len(links)
    any_spec = pl.BlockSpec(memory_space=pl.ANY)
    query_spec = pl.BlockSpec((cap, rows, width), lambda i, info: (0, 0, stage))
    out_spec = pl.BlockSpec((cap, rows, width + HD), lambda i, info: (0, 0, 0))
    return pl.pallas_call(
        partial(prompt_kernel, sub, members, links, cap, group_size),
        grid_spec=pltpu.PrefetchScalarGridSpec(
            num_scalar_prefetch=1,
            grid=(1,),
            in_specs=[any_spec] * len(chunks) + [query_spec] * count,
            out_specs=[out_spec] * count,
            scratch_shapes=[
                pltpu.VMEM((sub, members * tokens, HD), jnp.bfloat16),
                pltpu.VMEM((sub, members * tokens, HD), jnp.bfloat16),
                pltpu.SemaphoreType.DMA((sub, members, 2)),
            ],
        ),
        out_shape=[jax.ShapeDtypeStruct((cap, rows, width + HD), jnp.bfloat16)] * count,
        compiler_params=pltpu.CompilerParams(vmem_limit_bytes=40 * 1024 * 1024),
        cost_estimate=pl.CostEstimate(
            flops=cap * rows * width * members * tokens * 4 * sub,
            bytes_accessed=sub * members * tokens * HD * 4,
            transcendentals=cap * rows * group_size * members * tokens,
        ),
        name="prompt_attention",
    )(info, *chunks, *fetched)


def merge_kernel(sub, heads, links, cap, group_size, info_ref, *refs):
    count = len(links)
    query_ref, new_ref = refs[:2]
    result_refs = refs[2 : 2 + heads * count]
    out_ref = refs[-1]
    rows = query_ref.shape[1]
    wide = rows * group_size
    width = group_size * HD
    row_at = lax.broadcasted_iota(jnp.int32, (rows, rows), 0)
    token_at = lax.broadcasted_iota(jnp.int32, (rows, rows), 1)
    visible = (row_at // STEPS == token_at // STEPS) & (token_at <= row_at)
    visible = jnp.concatenate([visible.astype(jnp.int32)] * group_size, axis=0) > 0

    for i in range(sub):
        for h in range(heads):
            head = info_ref[cap + i] * heads + h
            columns = pl.ds(pl.multiple_of(head * width, width), width)
            new_columns = pl.ds(pl.multiple_of(head * HD, HD), HD)
            for c in range(cap):
                served = info_ref[c]
                raw = query_ref[c, :, columns]
                query = jnp.concatenate(
                    [raw[:, g * HD : (g + 1) * HD] for g in range(group_size)], axis=0
                )
                key = new_ref[0, c, :, new_columns]
                value = new_ref[1, c, :, new_columns]
                scores = lax.dot_general(
                    query, key, (((1,), (1,)), ((), ())), preferred_element_type=jnp.float32
                ) * HD ** -0.5
                scores = jnp.where(visible, scores, masked_score)
                peak = jnp.max(scores, axis=1, keepdims=True)
                weights = jnp.exp(scores - peak)
                total = jnp.sum(weights, axis=1, keepdims=True)
                own = lax.dot_general(
                    weights.astype(jnp.bfloat16), value, (((1,), (0,)), ((), ())),
                    preferred_element_type=jnp.float32,
                )
                chosen = None
                for n, (s, index) in enumerate(links):
                    if index != i:
                        continue
                    block = result_refs[h * count + n][c]
                    chosen = block if chosen is None else jnp.where(served == s, block, chosen)
                stats = chosen[:, width:].astype(jnp.float32)
                pieces = []
                for g in range(group_size):
                    span = slice(g * rows, (g + 1) * rows)
                    level = stats[:, g : g + 1] + stats[:, group_size + g : group_size + g + 1]
                    highest = jnp.maximum(level, peak[span])
                    scale = jnp.exp(level - highest)
                    own_scale = jnp.exp(peak[span] - highest)
                    inverse = 1.0 / (scale + total[span] * own_scale)
                    part = chosen[:, g * HD : (g + 1) * HD].astype(jnp.float32)
                    pieces.append((scale * inverse) * part + (own_scale * inverse) * own[span])
                out_ref[c, :, columns] = jnp.concatenate(pieces, axis=1).astype(jnp.bfloat16)


def merge_call(sub, heads, links, cap, group_size, info, queries, new_cache, results):
    full = lambda shape: pl.BlockSpec(shape, lambda i, info: (0,) * len(shape))
    return pl.pallas_call(
        partial(merge_kernel, sub, heads, links, cap, group_size),
        grid_spec=pltpu.PrefetchScalarGridSpec(
            num_scalar_prefetch=1,
            grid=(1,),
            in_specs=[full(queries.shape), full(new_cache.shape)] + [full(r.shape) for r in results],
            out_specs=full(queries.shape),
        ),
        out_shape=jax.ShapeDtypeStruct(queries.shape, jnp.bfloat16),
        compiler_params=pltpu.CompilerParams(vmem_limit_bytes=40 * 1024 * 1024),
        name="merge",
    )(info, queries, new_cache, *results)


def shards(prompt_cache, queries, new_cache, offsets, lengths, block_table):
    members = lax.axis_size("tensor")
    groups = lax.axis_size("group")
    cap = queries.shape[0]
    tokens = prompt_cache.shape[1]
    kv_local = prompt_cache.shape[2] // HD // members
    group_size = queries.shape[2] // (kv_local * HD)
    width = group_size * HD
    sub = TEAM if kv_local % TEAM == 0 and groups % TEAM == 0 else 1
    heads = kv_local // sub
    teams = groups // sub
    me = lax.axis_index("group").astype(jnp.int32)
    member = lax.axis_index("tensor").astype(jnp.int32)
    team, seat = me // sub, me % sub

    def device(team_at, seat_at, member_at):
        return ((team_at % teams) * sub + seat_at) * members + member_at % members

    def reaches(s, seat_at):
        return s * sub + seat_at - (sub - 1) <= REACH - 1

    links = []
    for s in range(REACH):
        if reaches(s, 0):
            links += [(s, i) for i in range(sub)]

    def pairs_of(s, i, back):
        pairs = []
        for a in range(teams):
            for b in range(sub):
                if reaches(s, b ^ i):
                    for m in range(members):
                        pair = (device(a + s, b ^ i, m), device(a, b, m))
                        pairs.append(pair[::-1] if back else pair)
        return pairs

    def to_prompt(value_of, s, i):
        value = value_of(seat ^ i)
        if s == 0 and i == 0:
            return value
        return lax.ppermute(value, AXES, pairs_of(s, i, False))

    meta = jnp.concatenate(
        [offsets.reshape(-1), lengths.reshape(-1), block_table.reshape(-1)]
    ).astype(jnp.int32)[None]
    metas = [to_prompt(lambda other: meta, s, i)[0] for s, i in links]

    def query_part(other):
        return lax.dynamic_slice_in_dim(queries, other * heads * width, heads * width, 2)

    def cache_part(j, r, h):
        other = ((member + r) % members) * kv_local + (seat ^ j) * heads + h
        part = lax.dynamic_slice_in_dim(prompt_cache, other * HD, HD, 2)
        if j == 0 and r == 0:
            return part
        pairs = [
            (device(a, b, m), device(a, b ^ j, m + r))
            for a in range(teams) for b in range(sub) for m in range(members)
        ]
        return lax.ppermute(part, AXES, pairs)

    fetched = [to_prompt(query_part, s, i) for s, i in links]
    stage_chunks = [
        [cache_part(j, r, h) for j in range(sub) for r in range(members)] for h in range(heads)
    ]

    per_member = tokens // BLOCK
    rows_info = []
    for j in range(sub):
        row = metas[j]
        table = row[cap + 1 :]
        order = ((member - table // per_member) % members) * per_member + table % per_member
        rows_info += [row[cap : cap + 1], order]
    wanted = []
    for n, (s, i) in enumerate(links):
        decode = (s * sub + (seat ^ i))
        prompt = decode - metas[n][:cap]
        here = (prompt >= 0) & (prompt < sub) & reaches(s, seat ^ i)
        wanted.append(jnp.where(here, prompt ^ seat, -1))
    info = jnp.concatenate(rows_info + wanted).astype(jnp.int32)

    results = []
    for h in range(heads):
        parts = prompt_call(
            sub, members, links, cap, group_size, h, info, stage_chunks[h], fetched
        )
        for n, (s, i) in enumerate(links):
            if s == 0 and i == 0:
                results.append(parts[n])
            else:
                results.append(lax.ppermute(parts[n], AXES, pairs_of(s, i, True)))

    own_offset = offsets.reshape(-1).astype(jnp.int32)
    served = jnp.where(own_offset <= seat, 0, (own_offset - seat + sub - 1) // sub)
    seats = jnp.stack([seat ^ i for i in range(sub)])
    merge_info = jnp.concatenate([served, seats]).astype(jnp.int32)
    return merge_call(sub, heads, links, cap, group_size, merge_info, queries, new_cache, results)


def solution(mesh):
    in_specs = (
        P(None, ("group", "tensor"), None),
        P("group", None, "tensor"),
        P(None, "group", None, "tensor"),
        P("group", None),
        P("group"),
        P("group", None),
    )
    out_specs = P("group", None, "tensor")
    return jax.shard_map(shards, mesh=mesh, in_specs=in_specs, out_specs=out_specs, check_vma=False)
```

```python
from functools import partial

import jax
import jax.numpy as jnp
from jax import lax
from jax.experimental import pallas as pl
from jax.experimental.pallas import tpu as pltpu
from jax.sharding import PartitionSpec as P


HD = 128
BLOCK = 128
STEPS = 4
REACH = 4
TEAM = 2
LADDER = (16, 8, 4)
PIECE = 128
LOG2E = 1.4426950408889634
AXES = ("group", "tensor")

masked_score = -1e30


def prompt_kernel(sub, members, links, cap, group_size, stage, info_ref, *refs):
    count = len(links)
    kv_refs = refs[: sub * members]
    query_refs = refs[sub * members : sub * members + count]
    out_refs = refs[sub * members + count : sub * members + 2 * count]
    keys, values, asked, answers, sems, query_sems, out_sems = refs[sub * members + 2 * count :]
    tokens = kv_refs[0].shape[1]
    rows = asked.shape[1]
    width = group_size * HD
    factor = HD ** -0.5 * LOG2E
    blocks = members * tokens // BLOCK
    per_piece = max(1, PIECE // rows)
    pieces = group_size // per_piece
    piece = per_piece * rows

    copies = []
    for j in range(sub):
        for r in range(members):
            source = kv_refs[j * members + r]
            for part, target in ((0, keys), (1, values)):
                copy = pltpu.make_async_copy(
                    source.at[part],
                    target.at[j, pl.ds(r * tokens, tokens), :],
                    sems.at[j, r, part],
                )
                copy.start()
                copies.append(copy)
    for n in range(count):
        copy = pltpu.make_async_copy(
            query_refs[n].at[:, :, pl.ds(stage * width, width)],
            asked.at[pl.ds(n * cap, cap)],
            query_sems.at[n],
        )
        copy.start()
        copies.append(copy)
    for copy in copies:
        copy.wait()

    lane = lax.broadcasted_iota(jnp.int32, (rows, HD), 1)

    def one(c, carry):
        j = info_ref[sub * (blocks + 1) + c]

        @pl.when(j >= 0)
        def _():
            base = j * (blocks + 1)
            length = info_ref[base]
            query = jnp.concatenate(
                [asked[c, :, g * HD : (g + 1) * HD] for g in range(group_size)], axis=0
            )

            def step(gather, masked, i, state):
                chunk = gather * BLOCK
                key_parts, value_parts = [], []
                for u in range(gather):
                    where = info_ref[base + 1 + i * gather + u]
                    rows_at = pl.ds(pl.multiple_of(where * BLOCK, BLOCK), BLOCK)
                    key_parts.append(keys[j, rows_at, :])
                    value_parts.append(values[j, rows_at, :])
                key = jnp.concatenate(key_parts, axis=0)
                value = jnp.concatenate(value_parts, axis=0)
                value = jnp.concatenate([value, jnp.ones_like(value)], axis=1)
                all_scores = [
                    lax.dot_general(
                        query[a * piece : (a + 1) * piece], key, (((1,), (1,)), ((), ())),
                        preferred_element_type=jnp.float32,
                    )
                    for a in range(pieces)
                ]
                result = []
                for scores, (peak, acc) in zip(all_scores, state):
                    if masked:
                        token = lax.broadcasted_iota(jnp.int32, (piece, chunk), 1)
                        scores = jnp.where(token < length - i * chunk, scores, masked_score)
                    new_peak = jnp.maximum(peak, jnp.max(scores, axis=1, keepdims=True))
                    weights = jnp.exp2(scores * factor - new_peak * factor)
                    decay = jnp.exp2(peak * factor - new_peak * factor)
                    acc = acc * decay + lax.dot_general(
                        weights.astype(jnp.bfloat16), value, (((1,), (0,)), ((), ())),
                        preferred_element_type=jnp.float32,
                    )
                    result.append((new_peak, acc))
                return tuple(result)

            state = tuple(
                (
                    jnp.full((piece, 1), masked_score, jnp.float32),
                    jnp.zeros((piece, 2 * HD), jnp.float32),
                )
                for _ in range(pieces)
            )
            done = 0
            for gather in LADDER:
                if blocks % gather:
                    continue
                chunk = gather * BLOCK
                start = done // chunk
                state = lax.fori_loop(
                    start, length // chunk, partial(step, gather, False), state
                )
                done = length // chunk * chunk
            start = done // chunk
            state = lax.fori_loop(
                start, (length + chunk - 1) // chunk, partial(step, gather, True), state
            )
            stats = jnp.zeros((rows, HD), jnp.float32)
            for a in range(pieces):
                peak, acc = state[a]
                total = acc[:, HD:]
                result = (acc[:, :HD] / total).astype(jnp.bfloat16)
                level = peak * HD ** -0.5 + jnp.log(total)
                for u in range(per_piece):
                    g = a * per_piece + u
                    span = slice(u * rows, (u + 1) * rows)
                    answers[c, :, g * HD : (g + 1) * HD] = result[span]
                    high = level[span].astype(jnp.bfloat16).astype(jnp.float32)
                    low = level[span] - high
                    stats = jnp.where(lane == g, high, stats)
                    stats = jnp.where(lane == group_size + g, low, stats)
            answers[c, :, group_size * HD :] = stats.astype(jnp.bfloat16)

        return carry

    lax.fori_loop(0, count * cap, one, 0)

    copies = []
    for n in range(count):
        copy = pltpu.make_async_copy(answers.at[pl.ds(n * cap, cap)], out_refs[n], out_sems.at[n])
        copy.start()
        copies.append(copy)
    for copy in copies:
        copy.wait()


def prompt_call(sub, members, links, cap, group_size, stage, info, chunks, fetched):
    rows = fetched[0].shape[1]
    tokens = chunks[0].shape[1]
    width = group_size * HD
    count = len(links)
    any_spec = pl.BlockSpec(memory_space=pl.ANY)
    return pl.pallas_call(
        partial(prompt_kernel, sub, members, links, cap, group_size, stage),
        grid_spec=pltpu.PrefetchScalarGridSpec(
            num_scalar_prefetch=1,
            grid=(1,),
            in_specs=[any_spec] * (len(chunks) + count),
            out_specs=[any_spec] * count,
            scratch_shapes=[
                pltpu.VMEM((sub, members * tokens, HD), jnp.bfloat16),
                pltpu.VMEM((sub, members * tokens, HD), jnp.bfloat16),
                pltpu.VMEM((count * cap, rows, width), jnp.bfloat16),
                pltpu.VMEM((count * cap, rows, width + HD), jnp.bfloat16),
                pltpu.SemaphoreType.DMA((sub, members, 2)),
                pltpu.SemaphoreType.DMA((count,)),
                pltpu.SemaphoreType.DMA((count,)),
            ],
        ),
        out_shape=[jax.ShapeDtypeStruct((cap, rows, width + HD), jnp.bfloat16)] * count,
        compiler_params=pltpu.CompilerParams(vmem_limit_bytes=40 * 1024 * 1024),
        cost_estimate=pl.CostEstimate(
            flops=cap * rows * width * members * tokens * 4 * sub,
            bytes_accessed=sub * members * tokens * HD * 4,
            transcendentals=cap * rows * group_size * members * tokens,
        ),
        name="prompt_attention",
    )(info, *chunks, *fetched)


def merge_kernel(sub, heads, h, links, cap, group_size, info_ref, *refs):
    count = len(links)
    query_ref, new_ref = refs[:2]
    result_refs = refs[2 : 2 + count]
    out_ref, buffer, sems = refs[-3:]
    rows = query_ref.shape[1]
    width = group_size * HD
    row_at = lax.broadcasted_iota(jnp.int32, (rows, rows), 0)
    token_at = lax.broadcasted_iota(jnp.int32, (rows, rows), 1)
    visible = (row_at // STEPS == token_at // STEPS) & (token_at <= row_at)
    visible = jnp.concatenate([visible.astype(jnp.int32)] * group_size, axis=0) > 0

    copies = []
    for i in range(sub):
        head = info_ref[cap + i] * heads + h
        columns = pl.ds(pl.multiple_of(head * width, width), width)
        new_columns = pl.ds(pl.multiple_of(head * HD, HD), HD)
        for c in range(cap):
            served = info_ref[c]
            raw = query_ref[c, :, columns]
            query = jnp.concatenate(
                [raw[:, g * HD : (g + 1) * HD] for g in range(group_size)], axis=0
            )
            key = new_ref[0, c, :, new_columns]
            value = new_ref[1, c, :, new_columns]
            scores = lax.dot_general(
                query, key, (((1,), (1,)), ((), ())), preferred_element_type=jnp.float32
            ) * HD ** -0.5
            scores = jnp.where(visible, scores, masked_score)
            peak = jnp.max(scores, axis=1, keepdims=True)
            weights = jnp.exp(scores - peak)
            total = jnp.sum(weights, axis=1, keepdims=True)
            own = lax.dot_general(
                weights.astype(jnp.bfloat16), value, (((1,), (0,)), ((), ())),
                preferred_element_type=jnp.float32,
            )
            chosen = None
            for n, (s, index) in enumerate(links):
                if index != i:
                    continue
                block = result_refs[n][c]
                chosen = block if chosen is None else jnp.where(served == s, block, chosen)
            stats = chosen[:, width:].astype(jnp.float32)
            pieces = []
            for g in range(group_size):
                span = slice(g * rows, (g + 1) * rows)
                level = stats[:, g : g + 1] + stats[:, group_size + g : group_size + g + 1]
                highest = jnp.maximum(level, peak[span])
                scale = jnp.exp(level - highest)
                own_scale = jnp.exp(peak[span] - highest)
                inverse = 1.0 / (scale + total[span] * own_scale)
                part = chosen[:, g * HD : (g + 1) * HD].astype(jnp.float32)
                pieces.append((scale * inverse) * part + (own_scale * inverse) * own[span])
            buffer[i, c] = jnp.concatenate(pieces, axis=1).astype(jnp.bfloat16)
            copy = pltpu.make_async_copy(buffer.at[i, c], out_ref.at[c, :, columns], sems.at[i, c])
            copy.start()
            copies.append(copy)
    for copy in copies:
        copy.wait()


def merge_call(sub, heads, h, links, cap, group_size, info, queries, new_cache, results, earlier):
    full = lambda shape: pl.BlockSpec(shape, lambda i, info: (0,) * len(shape))
    any_spec = pl.BlockSpec(memory_space=pl.ANY)
    rows = queries.shape[1]
    operands = [queries, new_cache, *results]
    specs = [full(x.shape) for x in operands]
    aliases = {}
    if earlier is not None:
        aliases = {1 + len(operands): 0}
        operands.append(earlier)
        specs.append(any_spec)
    return pl.pallas_call(
        partial(merge_kernel, sub, heads, h, links, cap, group_size),
        grid_spec=pltpu.PrefetchScalarGridSpec(
            num_scalar_prefetch=1,
            grid=(1,),
            in_specs=specs,
            out_specs=any_spec,
            scratch_shapes=[
                pltpu.VMEM((sub, cap, rows, group_size * HD), jnp.bfloat16),
                pltpu.SemaphoreType.DMA((sub, cap)),
            ],
        ),
        out_shape=jax.ShapeDtypeStruct(queries.shape, jnp.bfloat16),
        input_output_aliases=aliases,
        compiler_params=pltpu.CompilerParams(vmem_limit_bytes=40 * 1024 * 1024),
        cost_estimate=pl.CostEstimate(
            flops=sub * cap * rows * rows * group_size * HD * 4,
            bytes_accessed=8 * rows * cap * group_size * HD * sub,
            transcendentals=sub * cap * rows * rows * group_size,
        ),
        name="merge",
    )(info, *operands)


def shards(prompt_cache, queries, new_cache, offsets, lengths, block_table):
    members = lax.axis_size("tensor")
    groups = lax.axis_size("group")
    cap = queries.shape[0]
    tokens = prompt_cache.shape[1]
    kv_local = prompt_cache.shape[2] // HD // members
    group_size = queries.shape[2] // (kv_local * HD)
    width = group_size * HD
    sub = TEAM if kv_local % TEAM == 0 and groups % TEAM == 0 else 1
    heads = kv_local // sub
    teams = groups // sub
    me = lax.axis_index("group").astype(jnp.int32)
    member = lax.axis_index("tensor").astype(jnp.int32)
    seat = me % sub

    def device(team_at, seat_at, member_at):
        return ((team_at % teams) * sub + seat_at) * members + member_at % members

    def reaches(s, seat_at):
        return s * sub + seat_at - (sub - 1) <= REACH - 1

    links = []
    for s in range(REACH):
        if reaches(s, 0):
            links += [(s, i) for i in range(sub)]

    def pairs_of(s, i, back):
        pairs = []
        for a in range(teams):
            for b in range(sub):
                if reaches(s, b ^ i):
                    for m in range(members):
                        pair = (device(a + s, b ^ i, m), device(a, b, m))
                        pairs.append(pair[::-1] if back else pair)
        return pairs

    def to_prompt(value_of, s, i):
        value = value_of(seat ^ i)
        if s == 0 and i == 0:
            return value
        return lax.ppermute(value, AXES, pairs_of(s, i, False))

    meta = jnp.concatenate(
        [offsets.reshape(-1), lengths.reshape(-1), block_table.reshape(-1)]
    ).astype(jnp.int32)[None]
    metas = [to_prompt(lambda other: meta, s, i)[0] for s, i in links]

    def query_part(other):
        return lax.dynamic_slice_in_dim(queries, other * heads * width, heads * width, 2)

    def cache_slice(cache, j, r, h):
        other = ((member + r) % members) * kv_local + (seat ^ j) * heads + h
        return lax.dynamic_slice_in_dim(cache, other * HD, HD, 2)

    def cache_part(part, j, r):
        if j == 0 and r == 0:
            return part
        pairs = [
            (device(a, b, m), device(a, b ^ j, m + r))
            for a in range(teams) for b in range(sub) for m in range(members)
        ]
        return lax.ppermute(part, AXES, pairs)

    fetched = [to_prompt(query_part, s, i) for s, i in links]
    seats_of = [(j, r) for j in range(sub) for r in range(members)]
    stage_chunks = []
    cache = prompt_cache
    for h in range(heads):
        slices = [cache_slice(cache, j, r, h) for j, r in seats_of]
        cache, slices = lax.optimization_barrier((cache, slices))
        stage_chunks.append([cache_part(p, j, r) for p, (j, r) in zip(slices, seats_of)])

    per_member = tokens // BLOCK
    rows_info = []
    for j in range(sub):
        row = metas[j]
        table = row[cap + 1 :]
        order = ((member - table // per_member) % members) * per_member + table % per_member
        rows_info += [row[cap : cap + 1], order]
    wanted = []
    for n, (s, i) in enumerate(links):
        decode = (s * sub + (seat ^ i))
        prompt = decode - metas[n][:cap]
        here = (prompt >= 0) & (prompt < sub) & reaches(s, seat ^ i)
        wanted.append(jnp.where(here, prompt ^ seat, -1))
    info = jnp.concatenate(rows_info + wanted).astype(jnp.int32)

    own_offset = offsets.reshape(-1).astype(jnp.int32)
    served = jnp.where(own_offset <= seat, 0, (own_offset - seat + sub - 1) // sub)
    seats = jnp.stack([seat ^ i for i in range(sub)])
    merge_info = jnp.concatenate([served, seats]).astype(jnp.int32)
    output = None
    for h in range(heads):
        parts = prompt_call(
            sub, members, links, cap, group_size, h, info, stage_chunks[h], fetched
        )
        results = []
        for n, (s, i) in enumerate(links):
            if s == 0 and i == 0:
                results.append(parts[n])
            else:
                results.append(lax.ppermute(parts[n], AXES, pairs_of(s, i, True)))
        output = merge_call(
            sub, heads, h, links, cap, group_size, merge_info, queries, new_cache, results, output
        )
    return output


def solution(mesh):
    in_specs = (
        P(None, ("group", "tensor"), None),
        P("group", None, "tensor"),
        P(None, "group", None, "tensor"),
        P("group", None),
        P("group"),
        P("group", None),
    )
    out_specs = P("group", None, "tensor")

    return jax.shard_map(shards, mesh=mesh, in_specs=in_specs, out_specs=out_specs, check_vma=False)
```

```python
from functools import partial

import jax
import jax.numpy as jnp
from jax import lax
from jax.experimental import pallas as pl
from jax.experimental.pallas import tpu as pltpu
from jax.sharding import PartitionSpec as P


HD = 128
BLOCK = 128
STEPS = 4
REACH = 4
TEAM = 2
LADDER = (16, 8, 4)
PIECE = 128
LOG2E = 1.4426950408889634
AXES = ("group", "tensor")

masked_score = -1e30


def prompt_kernel(sub, members, links, cap, group_size, stage, last, blocks, info_ref, *refs):
    count = len(links)
    kv_refs = refs[: sub * members]
    query_refs = refs[sub * members : sub * members + count]
    if last:
        state_in = refs[sub * members + count]
        out_refs = refs[sub * members + count + 1 : sub * members + 2 * count + 1]
        keys, values, asked, kept, sems, query_sems, state_sem, answers, out_sems = refs[
            sub * members + 2 * count + 1 :
        ]
    else:
        state_out = refs[sub * members + count]
        keys, values, asked, kept, sems, query_sems, state_sem = refs[sub * members + count + 1 :]
    tokens = kv_refs[0].shape[1]
    rows = asked.shape[1]
    width = group_size * HD
    factor = HD ** -0.5 * LOG2E
    per_piece = max(1, PIECE // rows)
    pieces = group_size // per_piece
    piece = per_piece * rows

    def each_wanted(action):
        def visit(c, carry):
            @pl.when(info_ref[sub * (blocks + 1) + c] >= 0)
            def _():
                if last:
                    action(pltpu.make_async_copy(state_in.at[c], kept.at[c], state_sem.at[c]))
                else:
                    action(pltpu.make_async_copy(kept.at[c], state_out.at[c], state_sem.at[c]))

            return carry

        lax.fori_loop(0, count * cap, visit, 0)

    if last:
        each_wanted(lambda copy: copy.start())
    copies = []
    for j in range(sub):
        for r in range(members):
            source = kv_refs[j * members + r]
            for part, target in ((0, keys), (1, values)):
                copy = pltpu.make_async_copy(
                    source.at[part],
                    target.at[j, pl.ds(r * tokens, tokens), :],
                    sems.at[j, r, part],
                )
                copy.start()
                copies.append(copy)
    for n in range(count):
        copy = pltpu.make_async_copy(
            query_refs[n].at[:, :, pl.ds(stage * width, width)],
            asked.at[pl.ds(n * cap, cap)],
            query_sems.at[n],
        )
        copy.start()
        copies.append(copy)
    for copy in copies:
        copy.wait()
    if last:
        each_wanted(lambda copy: copy.wait())

    lane = lax.broadcasted_iota(jnp.int32, (rows, HD), 1)

    def one(c, carry):
        j = info_ref[sub * (blocks + 1) + c]

        @pl.when(j >= 0)
        def _():
            base = j * (blocks + 1)
            length = info_ref[base]
            query = jnp.concatenate(
                [asked[c, :, g * HD : (g + 1) * HD] for g in range(group_size)], axis=0
            )

            def step(gather, masked, i, state):
                chunk = gather * BLOCK
                key_parts, value_parts = [], []
                for u in range(gather):
                    where = info_ref[base + 1 + i * gather + u]
                    rows_at = pl.ds(pl.multiple_of(where * BLOCK, BLOCK), BLOCK)
                    key_parts.append(keys[j, rows_at, :])
                    value_parts.append(values[j, rows_at, :])
                key = jnp.concatenate(key_parts, axis=0)
                value = jnp.concatenate(value_parts, axis=0)
                value = jnp.concatenate([value, jnp.ones_like(value)], axis=1)
                all_scores = [
                    lax.dot_general(
                        query[a * piece : (a + 1) * piece], key, (((1,), (1,)), ((), ())),
                        preferred_element_type=jnp.float32,
                    )
                    for a in range(pieces)
                ]
                result = []
                for scores, (peak, acc) in zip(all_scores, state):
                    if masked:
                        token = lax.broadcasted_iota(jnp.int32, (piece, chunk), 1)
                        scores = jnp.where(token < length - i * chunk, scores, masked_score)
                    new_peak = jnp.maximum(peak, jnp.max(scores, axis=1, keepdims=True))
                    weights = jnp.exp2(scores * factor - new_peak * factor)
                    decay = jnp.exp2(peak * factor - new_peak * factor)
                    acc = acc * decay + lax.dot_general(
                        weights.astype(jnp.bfloat16), value, (((1,), (0,)), ((), ())),
                        preferred_element_type=jnp.float32,
                    )
                    result.append((new_peak, acc))
                return tuple(result)

            if last:
                state = []
                for a in range(pieces):
                    whole = kept[c, a * piece : (a + 1) * piece, :]
                    peak = whole[:, 2 * HD - 1 :]
                    total = jnp.broadcast_to(whole[:, HD : HD + 1], (piece, HD))
                    state.append((peak, jnp.concatenate([whole[:, :HD], total], axis=1)))
                state = tuple(state)
            else:
                state = tuple(
                    (
                        jnp.full((piece, 1), masked_score, jnp.float32),
                        jnp.zeros((piece, 2 * HD), jnp.float32),
                    )
                    for _ in range(pieces)
                )
            done = 0
            for gather in LADDER:
                if blocks % gather:
                    continue
                chunk = gather * BLOCK
                start = done // chunk
                state = lax.fori_loop(
                    start, length // chunk, partial(step, gather, False), state
                )
                done = length // chunk * chunk
            start = done // chunk
            state = lax.fori_loop(
                start, (length + chunk - 1) // chunk, partial(step, gather, True), state
            )
            if not last:
                side = lax.broadcasted_iota(jnp.int32, (piece, HD), 1)
                for a in range(pieces):
                    peak, acc = state[a]
                    tail = jnp.where(side < HD // 2, acc[:, HD:], peak)
                    kept[c, a * piece : (a + 1) * piece, :] = jnp.concatenate(
                        [acc[:, :HD], tail], axis=1
                    )
                pltpu.make_async_copy(kept.at[c], state_out.at[c], state_sem.at[c]).start()
                return
            stats = jnp.zeros((rows, HD), jnp.float32)
            for a in range(pieces):
                peak, acc = state[a]
                total = acc[:, HD:]
                result = (acc[:, :HD] / total).astype(jnp.bfloat16)
                level = peak * HD ** -0.5 + jnp.log(total)
                for u in range(per_piece):
                    g = a * per_piece + u
                    span = slice(u * rows, (u + 1) * rows)
                    answers[c, :, g * HD : (g + 1) * HD] = result[span]
                    high = level[span].astype(jnp.bfloat16).astype(jnp.float32)
                    low = level[span] - high
                    stats = jnp.where(lane == g, high, stats)
                    stats = jnp.where(lane == group_size + g, low, stats)
            answers[c, :, group_size * HD :] = stats.astype(jnp.bfloat16)

        return carry

    lax.fori_loop(0, count * cap, one, 0)
    if not last:
        each_wanted(lambda copy: copy.wait())
        return

    copies = []
    for n in range(count):
        copy = pltpu.make_async_copy(answers.at[pl.ds(n * cap, cap)], out_refs[n], out_sems.at[n])
        copy.start()
        copies.append(copy)
    for copy in copies:
        copy.wait()


def prompt_call(sub, links, cap, group_size, stage, blocks, info, chunks, fetched, state):
    last = state is not None
    rows = fetched[0].shape[1]
    tokens = chunks[0].shape[1]
    members = len(chunks) // sub
    width = group_size * HD
    count = len(links)
    any_spec = pl.BlockSpec(memory_space=pl.ANY)
    state_shape = (count * cap, rows * group_size, 2 * HD)
    scratch = [
        pltpu.VMEM((sub, members * tokens, HD), jnp.bfloat16),
        pltpu.VMEM((sub, members * tokens, HD), jnp.bfloat16),
        pltpu.VMEM((count * cap, rows, width), jnp.bfloat16),
        pltpu.VMEM(state_shape, jnp.float32),
        pltpu.SemaphoreType.DMA((sub, members, 2)),
        pltpu.SemaphoreType.DMA((count,)),
        pltpu.SemaphoreType.DMA((count * cap,)),
    ]
    operands = [*chunks, *fetched]
    if last:
        operands.append(state)
        scratch += [
            pltpu.VMEM((count * cap, rows, width + HD), jnp.bfloat16),
            pltpu.SemaphoreType.DMA((count,)),
        ]
        out_shape = [jax.ShapeDtypeStruct((cap, rows, width + HD), jnp.bfloat16)] * count
    else:
        out_shape = [jax.ShapeDtypeStruct(state_shape, jnp.float32)]
    return pl.pallas_call(
        partial(prompt_kernel, sub, members, links, cap, group_size, stage, last, blocks),
        grid_spec=pltpu.PrefetchScalarGridSpec(
            num_scalar_prefetch=1,
            grid=(1,),
            in_specs=[any_spec] * len(operands),
            out_specs=[any_spec] * len(out_shape),
            scratch_shapes=scratch,
        ),
        out_shape=out_shape,
        compiler_params=pltpu.CompilerParams(vmem_limit_bytes=48 * 1024 * 1024),
        cost_estimate=pl.CostEstimate(
            flops=cap * rows * width * members * tokens * 4 * sub,
            bytes_accessed=sub * members * tokens * HD * 4,
            transcendentals=cap * rows * group_size * members * tokens,
        ),
        name="prompt_last" if last else "prompt_first",
    )(info, *operands)


def merge_kernel(sub, heads, h, links, cap, group_size, info_ref, *refs):
    count = len(links)
    query_ref, new_ref = refs[:2]
    result_refs = refs[2 : 2 + count]
    out_ref, buffer, sems = refs[-3:]
    rows = query_ref.shape[1]
    width = group_size * HD
    row_at = lax.broadcasted_iota(jnp.int32, (rows, rows), 0)
    token_at = lax.broadcasted_iota(jnp.int32, (rows, rows), 1)
    visible = (row_at // STEPS == token_at // STEPS) & (token_at <= row_at)
    visible = jnp.concatenate([visible.astype(jnp.int32)] * group_size, axis=0) > 0

    copies = []
    for i in range(sub):
        head = info_ref[cap + i] * heads + h
        columns = pl.ds(pl.multiple_of(head * width, width), width)
        new_columns = pl.ds(pl.multiple_of(head * HD, HD), HD)
        for c in range(cap):
            served = info_ref[c]
            raw = query_ref[c, :, columns]
            query = jnp.concatenate(
                [raw[:, g * HD : (g + 1) * HD] for g in range(group_size)], axis=0
            )
            key = new_ref[0, c, :, new_columns]
            value = new_ref[1, c, :, new_columns]
            scores = lax.dot_general(
                query, key, (((1,), (1,)), ((), ())), preferred_element_type=jnp.float32
            ) * HD ** -0.5
            scores = jnp.where(visible, scores, masked_score)
            peak = jnp.max(scores, axis=1, keepdims=True)
            weights = jnp.exp(scores - peak)
            total = jnp.sum(weights, axis=1, keepdims=True)
            own = lax.dot_general(
                weights.astype(jnp.bfloat16), value, (((1,), (0,)), ((), ())),
                preferred_element_type=jnp.float32,
            )
            chosen = None
            for n, (s, index) in enumerate(links):
                if index != i:
                    continue
                block = result_refs[n][c]
                chosen = block if chosen is None else jnp.where(served == s, block, chosen)
            stats = chosen[:, width:].astype(jnp.float32)
            pieces = []
            for g in range(group_size):
                span = slice(g * rows, (g + 1) * rows)
                level = stats[:, g : g + 1] + stats[:, group_size + g : group_size + g + 1]
                highest = jnp.maximum(level, peak[span])
                scale = jnp.exp(level - highest)
                own_scale = jnp.exp(peak[span] - highest)
                inverse = 1.0 / (scale + total[span] * own_scale)
                part = chosen[:, g * HD : (g + 1) * HD].astype(jnp.float32)
                pieces.append((scale * inverse) * part + (own_scale * inverse) * own[span])
            buffer[i, c] = jnp.concatenate(pieces, axis=1).astype(jnp.bfloat16)
            copy = pltpu.make_async_copy(buffer.at[i, c], out_ref.at[c, :, columns], sems.at[i, c])
            copy.start()
            copies.append(copy)
    for copy in copies:
        copy.wait()


def merge_call(sub, heads, h, links, cap, group_size, info, queries, new_cache, results, earlier):
    full = lambda shape: pl.BlockSpec(shape, lambda i, info: (0,) * len(shape))
    any_spec = pl.BlockSpec(memory_space=pl.ANY)
    rows = queries.shape[1]
    operands = [queries, new_cache, *results]
    specs = [full(x.shape) for x in operands]
    aliases = {}
    if earlier is not None:
        aliases = {1 + len(operands): 0}
        operands.append(earlier)
        specs.append(any_spec)
    return pl.pallas_call(
        partial(merge_kernel, sub, heads, h, links, cap, group_size),
        grid_spec=pltpu.PrefetchScalarGridSpec(
            num_scalar_prefetch=1,
            grid=(1,),
            in_specs=specs,
            out_specs=any_spec,
            scratch_shapes=[
                pltpu.VMEM((sub, cap, rows, group_size * HD), jnp.bfloat16),
                pltpu.SemaphoreType.DMA((sub, cap)),
            ],
        ),
        out_shape=jax.ShapeDtypeStruct(queries.shape, jnp.bfloat16),
        input_output_aliases=aliases,
        compiler_params=pltpu.CompilerParams(vmem_limit_bytes=40 * 1024 * 1024),
        cost_estimate=pl.CostEstimate(
            flops=sub * cap * rows * rows * group_size * HD * 4,
            bytes_accessed=8 * rows * cap * group_size * HD * sub,
            transcendentals=sub * cap * rows * rows * group_size,
        ),
        name="merge",
    )(info, *operands)


def shards(prompt_cache, queries, new_cache, offsets, lengths, block_table):
    members = lax.axis_size("tensor")
    groups = lax.axis_size("group")
    cap = queries.shape[0]
    tokens = prompt_cache.shape[1]
    kv_local = prompt_cache.shape[2] // HD // members
    group_size = queries.shape[2] // (kv_local * HD)
    width = group_size * HD
    sub = TEAM if kv_local % TEAM == 0 and groups % TEAM == 0 else 1
    heads = kv_local // sub
    teams = groups // sub
    me = lax.axis_index("group").astype(jnp.int32)
    member = lax.axis_index("tensor").astype(jnp.int32)
    seat = me % sub

    def device(team_at, seat_at, member_at):
        return ((team_at % teams) * sub + seat_at) * members + member_at % members

    def reaches(s, seat_at):
        return s * sub + seat_at - (sub - 1) <= REACH - 1

    links = []
    for s in range(REACH):
        if reaches(s, 0):
            links += [(s, i) for i in range(sub)]

    def pairs_of(s, i, back):
        pairs = []
        for a in range(teams):
            for b in range(sub):
                if reaches(s, b ^ i):
                    for m in range(members):
                        pair = (device(a + s, b ^ i, m), device(a, b, m))
                        pairs.append(pair[::-1] if back else pair)
        return pairs

    def to_prompt(value_of, s, i):
        value = value_of(seat ^ i)
        if s == 0 and i == 0:
            return value
        return lax.ppermute(value, AXES, pairs_of(s, i, False))

    meta = jnp.concatenate(
        [offsets.reshape(-1), lengths.reshape(-1), block_table.reshape(-1)]
    ).astype(jnp.int32)[None]
    metas = [to_prompt(lambda other: meta, s, i)[0] for s, i in links]

    def query_part(other):
        return lax.dynamic_slice_in_dim(queries, other * heads * width, heads * width, 2)

    def cache_slice(cache, j, r, h):
        other = ((member + r) % members) * kv_local + (seat ^ j) * heads + h
        return lax.dynamic_slice_in_dim(cache, other * HD, HD, 2)

    def cache_part(part, j, r):
        if j == 0 and r == 0:
            return part
        pairs = [
            (device(a, b, m), device(a, b ^ j, m + r))
            for a in range(teams) for b in range(sub) for m in range(members)
        ]
        return lax.ppermute(part, AXES, pairs)

    fetched = [to_prompt(query_part, s, i) for s, i in links]
    seats_of = [(j, r) for j in range(sub) for r in range(members)]
    stage_chunks = []
    cache = prompt_cache
    for h in range(heads):
        slices = [cache_slice(cache, j, r, h) for j, r in seats_of]
        cache, slices = lax.optimization_barrier((cache, slices))
        stage_chunks.append([cache_part(p, j, r) for p, (j, r) in zip(slices, seats_of)])

    per_member = tokens // BLOCK
    blocks = block_table.shape[1]
    logical = jnp.arange(blocks, dtype=jnp.int32)
    wanted = []
    for n, (s, i) in enumerate(links):
        decode = s * sub + (seat ^ i)
        prompt = decode - metas[n][:cap]
        here = (prompt >= 0) & (prompt < sub) & reaches(s, seat ^ i)
        wanted.append(jnp.where(here, prompt ^ seat, -1))
    infos = []
    for last in (False, True):
        rows_info = []
        for j in range(sub):
            length, table = metas[j][cap], metas[j][cap + 1 :]
            turn = (member - table // per_member) % members
            mine = (turn > 0) if last else (turn == 0)
            place = (turn - 1 if last else turn) * per_member + table % per_member
            live = jnp.clip(length - logical * BLOCK, 0, BLOCK)
            rank = jnp.sum((mine[None, :] & (logical[None, :] < logical[:, None])), axis=1)
            chosen = mine[:, None] & (rank[:, None] == logical[None, :])
            rows_info.append(jnp.sum(jnp.where(mine, live, 0))[None])
            rows_info.append(jnp.sum(jnp.where(chosen, place[:, None], 0), axis=0))
        infos.append(jnp.concatenate(rows_info + wanted).astype(jnp.int32))

    own_offset = offsets.reshape(-1).astype(jnp.int32)
    served = jnp.where(own_offset <= seat, 0, (own_offset - seat + sub - 1) // sub)
    seats = jnp.stack([seat ^ i for i in range(sub)])
    merge_info = jnp.concatenate([served, seats]).astype(jnp.int32)
    output = None
    near_chunks, far_chunks = [], []
    for chunks in stage_chunks:
        near_chunks.append([chunks[n] for n, (j, r) in enumerate(seats_of) if r == 0])
        far_chunks.append([chunks[n] for n, (j, r) in enumerate(seats_of) if r > 0])
    states = [
        prompt_call(
            sub, links, cap, group_size, h, blocks, infos[0], near_chunks[h], fetched, None
        )[0]
        for h in range(heads)
    ]
    states = lax.optimization_barrier(states)
    for h in range(heads):
        parts = prompt_call(
            sub, links, cap, group_size, h, blocks, infos[1], far_chunks[h], fetched, states[h]
        )
        results = []
        for n, (s, i) in enumerate(links):
            if s == 0 and i == 0:
                results.append(parts[n])
            else:
                results.append(lax.ppermute(parts[n], AXES, pairs_of(s, i, True)))
        output = merge_call(
            sub, heads, h, links, cap, group_size, merge_info, queries, new_cache, results, output
        )
    return output


def solution(mesh):
    in_specs = (
        P(None, ("group", "tensor"), None),
        P("group", None, "tensor"),
        P(None, "group", None, "tensor"),
        P("group", None),
        P("group"),
        P("group", None),
    )
    out_specs = P("group", None, "tensor")

    return jax.shard_map(shards, mesh=mesh, in_specs=in_specs, out_specs=out_specs, check_vma=False)
```

```python
from functools import partial

import jax
import jax.numpy as jnp
from jax import lax
from jax.experimental import pallas as pl
from jax.experimental.pallas import tpu as pltpu
from jax.sharding import PartitionSpec as P


HD = 128
BLOCK = 128
STEPS = 4
REACH = 4
TEAM = 2
LADDER = (16, 8, 4)
PIECE = 128
LOG2E = 1.4426950408889634
AXES = ("group", "tensor")

masked_score = -1e30


def prompt_kernel(sub, members, links, cap, group_size, last, blocks, info_ref, *refs):
    count = len(links)
    kv_refs = refs[: sub * members]
    query_refs = refs[sub * members : sub * members + count]
    if last:
        state_in = refs[sub * members + count]
        out_refs = refs[sub * members + count + 1 : sub * members + 2 * count + 1]
        keys, values, asked, kept, sems, query_sems, state_sem, answers, out_sems = refs[
            sub * members + 2 * count + 1 :
        ]
    else:
        state_out = refs[sub * members + count]
        keys, values, asked, kept, sems, query_sems, state_sem = refs[sub * members + count + 1 :]
    tokens = kv_refs[0].shape[1]
    rows = asked.shape[1]
    factor = HD ** -0.5 * LOG2E
    per_piece = max(1, PIECE // rows)
    pieces = group_size // per_piece
    piece = per_piece * rows

    def each_wanted(action):
        def visit(c, carry):
            @pl.when(info_ref[sub * (blocks + 1) + c] >= 0)
            def _():
                if last:
                    action(pltpu.make_async_copy(state_in.at[c], kept.at[c], state_sem.at[c]))
                else:
                    action(pltpu.make_async_copy(kept.at[c], state_out.at[c], state_sem.at[c]))

            return carry

        lax.fori_loop(0, count * cap, visit, 0)

    if last:
        each_wanted(lambda copy: copy.start())
    copies = []
    for j in range(sub):
        for r in range(members):
            source = kv_refs[j * members + r]
            for part, target in ((0, keys), (1, values)):
                copy = pltpu.make_async_copy(
                    source.at[part],
                    target.at[j, pl.ds(r * tokens, tokens), :],
                    sems.at[j, r, part],
                )
                copy.start()
                copies.append(copy)
    for n in range(count):
        copy = pltpu.make_async_copy(
            query_refs[n],
            asked.at[pl.ds(n * cap, cap)],
            query_sems.at[n],
        )
        copy.start()
        copies.append(copy)
    for copy in copies:
        copy.wait()
    if last:
        each_wanted(lambda copy: copy.wait())

    lane = lax.broadcasted_iota(jnp.int32, (rows, HD), 1)

    def one(c, carry):
        j = info_ref[sub * (blocks + 1) + c]

        @pl.when(j >= 0)
        def _():
            base = j * (blocks + 1)
            length = info_ref[base]
            query = jnp.concatenate(
                [asked[c, :, g * HD : (g + 1) * HD] for g in range(group_size)], axis=0
            )

            def step(gather, masked, i, state):
                chunk = gather * BLOCK
                key_parts, value_parts = [], []
                for u in range(gather):
                    where = info_ref[base + 1 + i * gather + u]
                    rows_at = pl.ds(pl.multiple_of(where * BLOCK, BLOCK), BLOCK)
                    key_parts.append(keys[j, rows_at, :])
                    value_parts.append(values[j, rows_at, :])
                key = jnp.concatenate(key_parts, axis=0)
                value = jnp.concatenate(value_parts, axis=0)
                value = jnp.concatenate([value, jnp.ones_like(value)], axis=1)
                all_scores = [
                    lax.dot_general(
                        query[a * piece : (a + 1) * piece], key, (((1,), (1,)), ((), ())),
                        preferred_element_type=jnp.float32,
                    )
                    for a in range(pieces)
                ]
                result = []
                for scores, (peak, acc) in zip(all_scores, state):
                    if masked:
                        token = lax.broadcasted_iota(jnp.int32, (piece, chunk), 1)
                        scores = jnp.where(token < length - i * chunk, scores, masked_score)
                    new_peak = jnp.maximum(peak, jnp.max(scores, axis=1, keepdims=True))
                    weights = jnp.exp2(scores * factor - new_peak * factor)
                    decay = jnp.exp2(peak * factor - new_peak * factor)
                    acc = acc * decay + lax.dot_general(
                        weights.astype(jnp.bfloat16), value, (((1,), (0,)), ((), ())),
                        preferred_element_type=jnp.float32,
                    )
                    result.append((new_peak, acc))
                return tuple(result)

            if last:
                state = []
                for a in range(pieces):
                    whole = kept[c, a * piece : (a + 1) * piece, :]
                    peak = whole[:, 2 * HD - 1 :]
                    total = jnp.broadcast_to(whole[:, HD : HD + 1], (piece, HD))
                    state.append((peak, jnp.concatenate([whole[:, :HD], total], axis=1)))
                state = tuple(state)
            else:
                state = tuple(
                    (
                        jnp.full((piece, 1), masked_score, jnp.float32),
                        jnp.zeros((piece, 2 * HD), jnp.float32),
                    )
                    for _ in range(pieces)
                )
            done = 0
            for gather in LADDER:
                if blocks % gather:
                    continue
                chunk = gather * BLOCK
                start = done // chunk
                state = lax.fori_loop(
                    start, length // chunk, partial(step, gather, False), state
                )
                done = length // chunk * chunk
            start = done // chunk
            state = lax.fori_loop(
                start, (length + chunk - 1) // chunk, partial(step, gather, True), state
            )
            if not last:
                side = lax.broadcasted_iota(jnp.int32, (piece, HD), 1)
                for a in range(pieces):
                    peak, acc = state[a]
                    tail = jnp.where(side < HD // 2, acc[:, HD:], peak)
                    kept[c, a * piece : (a + 1) * piece, :] = jnp.concatenate(
                        [acc[:, :HD], tail], axis=1
                    )
                pltpu.make_async_copy(kept.at[c], state_out.at[c], state_sem.at[c]).start()
                return
            stats = jnp.zeros((rows, HD), jnp.float32)
            for a in range(pieces):
                peak, acc = state[a]
                total = acc[:, HD:]
                result = (acc[:, :HD] / total).astype(jnp.bfloat16)
                level = peak * HD ** -0.5 + jnp.log(total)
                for u in range(per_piece):
                    g = a * per_piece + u
                    span = slice(u * rows, (u + 1) * rows)
                    answers[c, :, g * HD : (g + 1) * HD] = result[span]
                    high = level[span].astype(jnp.bfloat16).astype(jnp.float32)
                    low = level[span] - high
                    stats = jnp.where(lane == g, high, stats)
                    stats = jnp.where(lane == group_size + g, low, stats)
            answers[c, :, group_size * HD :] = stats.astype(jnp.bfloat16)

        return carry

    lax.fori_loop(0, count * cap, one, 0)
    if not last:
        each_wanted(lambda copy: copy.wait())
        return

    copies = []
    for n in range(count):
        copy = pltpu.make_async_copy(answers.at[pl.ds(n * cap, cap)], out_refs[n], out_sems.at[n])
        copy.start()
        copies.append(copy)
    for copy in copies:
        copy.wait()


def prompt_call(sub, links, cap, group_size, blocks, info, chunks, fetched, state):
    last = state is not None
    rows = fetched[0].shape[1]
    tokens = chunks[0].shape[1]
    members = len(chunks) // sub
    width = group_size * HD
    count = len(links)
    any_spec = pl.BlockSpec(memory_space=pl.ANY)
    state_shape = (count * cap, rows * group_size, 2 * HD)
    scratch = [
        pltpu.VMEM((sub, members * tokens, HD), jnp.bfloat16),
        pltpu.VMEM((sub, members * tokens, HD), jnp.bfloat16),
        pltpu.VMEM((count * cap, rows, width), jnp.bfloat16),
        pltpu.VMEM(state_shape, jnp.float32),
        pltpu.SemaphoreType.DMA((sub, members, 2)),
        pltpu.SemaphoreType.DMA((count,)),
        pltpu.SemaphoreType.DMA((count * cap,)),
    ]
    operands = [*chunks, *fetched]
    if last:
        operands.append(state)
        scratch += [
            pltpu.VMEM((count * cap, rows, width + HD), jnp.bfloat16),
            pltpu.SemaphoreType.DMA((count,)),
        ]
        out_shape = [jax.ShapeDtypeStruct((cap, rows, width + HD), jnp.bfloat16)] * count
    else:
        out_shape = [jax.ShapeDtypeStruct(state_shape, jnp.float32)]
    return pl.pallas_call(
        partial(prompt_kernel, sub, members, links, cap, group_size, last, blocks),
        grid_spec=pltpu.PrefetchScalarGridSpec(
            num_scalar_prefetch=1,
            grid=(1,),
            in_specs=[any_spec] * len(operands),
            out_specs=[any_spec] * len(out_shape),
            scratch_shapes=scratch,
        ),
        out_shape=out_shape,
        compiler_params=pltpu.CompilerParams(vmem_limit_bytes=48 * 1024 * 1024),
        cost_estimate=pl.CostEstimate(
            flops=cap * rows * width * members * tokens * 4 * sub,
            bytes_accessed=sub * members * tokens * HD * 4,
            transcendentals=cap * rows * group_size * members * tokens,
        ),
        name="prompt_last" if last else "prompt_first",
    )(info, *operands)


def merge_kernel(sub, heads, h, links, cap, group_size, info_ref, *refs):
    count = len(links)
    query_ref, new_ref = refs[:2]
    result_refs = refs[2 : 2 + count]
    out_ref, buffer, sems = refs[-3:]
    rows = query_ref.shape[1]
    width = group_size * HD
    row_at = lax.broadcasted_iota(jnp.int32, (rows, rows), 0)
    token_at = lax.broadcasted_iota(jnp.int32, (rows, rows), 1)
    visible = (row_at // STEPS == token_at // STEPS) & (token_at <= row_at)
    visible = jnp.concatenate([visible.astype(jnp.int32)] * group_size, axis=0) > 0

    copies = []
    for i in range(sub):
        head = info_ref[cap + i] * heads + h
        columns = pl.ds(pl.multiple_of(head * width, width), width)
        new_columns = pl.ds(pl.multiple_of(head * HD, HD), HD)
        for c in range(cap):
            served = info_ref[c]
            raw = query_ref[c, :, columns]
            query = jnp.concatenate(
                [raw[:, g * HD : (g + 1) * HD] for g in range(group_size)], axis=0
            )
            key = new_ref[0, c, :, new_columns]
            value = new_ref[1, c, :, new_columns]
            scores = lax.dot_general(
                query, key, (((1,), (1,)), ((), ())), preferred_element_type=jnp.float32
            ) * HD ** -0.5
            scores = jnp.where(visible, scores, masked_score)
            peak = jnp.max(scores, axis=1, keepdims=True)
            weights = jnp.exp(scores - peak)
            total = jnp.sum(weights, axis=1, keepdims=True)
            own = lax.dot_general(
                weights.astype(jnp.bfloat16), value, (((1,), (0,)), ((), ())),
                preferred_element_type=jnp.float32,
            )
            chosen = None
            for n, (s, index) in enumerate(links):
                if index != i:
                    continue
                block = result_refs[n][c]
                chosen = block if chosen is None else jnp.where(served == s, block, chosen)
            stats = chosen[:, width:].astype(jnp.float32)
            pieces = []
            for g in range(group_size):
                span = slice(g * rows, (g + 1) * rows)
                level = stats[:, g : g + 1] + stats[:, group_size + g : group_size + g + 1]
                highest = jnp.maximum(level, peak[span])
                scale = jnp.exp(level - highest)
                own_scale = jnp.exp(peak[span] - highest)
                inverse = 1.0 / (scale + total[span] * own_scale)
                part = chosen[:, g * HD : (g + 1) * HD].astype(jnp.float32)
                pieces.append((scale * inverse) * part + (own_scale * inverse) * own[span])
            buffer[i, c] = jnp.concatenate(pieces, axis=1).astype(jnp.bfloat16)
            copy = pltpu.make_async_copy(buffer.at[i, c], out_ref.at[c, :, columns], sems.at[i, c])
            copy.start()
            copies.append(copy)
    for copy in copies:
        copy.wait()


def merge_call(sub, heads, h, links, cap, group_size, info, queries, new_cache, results, earlier):
    full = lambda shape: pl.BlockSpec(shape, lambda i, info: (0,) * len(shape))
    any_spec = pl.BlockSpec(memory_space=pl.ANY)
    rows = queries.shape[1]
    operands = [queries, new_cache, *results]
    specs = [full(x.shape) for x in operands]
    aliases = {}
    if earlier is not None:
        aliases = {1 + len(operands): 0}
        operands.append(earlier)
        specs.append(any_spec)
    return pl.pallas_call(
        partial(merge_kernel, sub, heads, h, links, cap, group_size),
        grid_spec=pltpu.PrefetchScalarGridSpec(
            num_scalar_prefetch=1,
            grid=(1,),
            in_specs=specs,
            out_specs=any_spec,
            scratch_shapes=[
                pltpu.VMEM((sub, cap, rows, group_size * HD), jnp.bfloat16),
                pltpu.SemaphoreType.DMA((sub, cap)),
            ],
        ),
        out_shape=jax.ShapeDtypeStruct(queries.shape, jnp.bfloat16),
        input_output_aliases=aliases,
        compiler_params=pltpu.CompilerParams(vmem_limit_bytes=40 * 1024 * 1024),
        cost_estimate=pl.CostEstimate(
            flops=sub * cap * rows * rows * group_size * HD * 4,
            bytes_accessed=8 * rows * cap * group_size * HD * sub,
            transcendentals=sub * cap * rows * rows * group_size,
        ),
        name="merge",
    )(info, *operands)


def shards(prompt_cache, queries, new_cache, offsets, lengths, block_table):
    members = lax.axis_size("tensor")
    groups = lax.axis_size("group")
    cap = queries.shape[0]
    tokens = prompt_cache.shape[1]
    kv_local = prompt_cache.shape[2] // HD // members
    group_size = queries.shape[2] // (kv_local * HD)
    width = group_size * HD
    sub = TEAM if kv_local % TEAM == 0 and groups % TEAM == 0 else 1
    heads = kv_local // sub
    teams = groups // sub
    me = lax.axis_index("group").astype(jnp.int32)
    member = lax.axis_index("tensor").astype(jnp.int32)
    seat = me % sub

    def device(team_at, seat_at, member_at):
        return ((team_at % teams) * sub + seat_at) * members + member_at % members

    def reaches(s, seat_at):
        return s * sub + seat_at - (sub - 1) <= REACH - 1

    links = []
    for s in range(REACH):
        if reaches(s, 0):
            links += [(s, i) for i in range(sub)]

    def pairs_of(s, i, back):
        pairs = []
        for a in range(teams):
            for b in range(sub):
                if reaches(s, b ^ i):
                    for m in range(members):
                        pair = (device(a + s, b ^ i, m), device(a, b, m))
                        pairs.append(pair[::-1] if back else pair)
        return pairs

    def to_prompt(value_of, s, i):
        value = value_of(seat ^ i)
        if s == 0 and i == 0:
            return value
        return lax.ppermute(value, AXES, pairs_of(s, i, False))

    meta = jnp.concatenate(
        [offsets.reshape(-1), lengths.reshape(-1), block_table.reshape(-1)]
    ).astype(jnp.int32)[None]
    metas = [to_prompt(lambda other: meta, s, i)[0] for s, i in links]

    def query_part(h, other):
        return lax.dynamic_slice_in_dim(queries, (other * heads + h) * width, width, 2)

    def cache_slice(cache, j, r, h):
        other = ((member + r) % members) * kv_local + (seat ^ j) * heads + h
        return lax.dynamic_slice_in_dim(cache, other * HD, HD, 2)

    def cache_part(part, j, r):
        if j == 0 and r == 0:
            return part
        pairs = [
            (device(a, b, m), device(a, b ^ j, m + r))
            for a in range(teams) for b in range(sub) for m in range(members)
        ]
        return lax.ppermute(part, AXES, pairs)

    fetched = [[to_prompt(partial(query_part, h), s, i) for s, i in links] for h in range(heads)]
    seats_of = [(j, r) for j in range(sub) for r in range(members)]
    stage_chunks = []
    cache = prompt_cache
    for h in range(heads):
        slices = [cache_slice(cache, j, r, h) for j, r in seats_of]
        cache, slices = lax.optimization_barrier((cache, slices))
        stage_chunks.append([cache_part(p, j, r) for p, (j, r) in zip(slices, seats_of)])

    per_member = tokens // BLOCK
    blocks = block_table.shape[1]
    logical = jnp.arange(blocks, dtype=jnp.int32)
    wanted = []
    for n, (s, i) in enumerate(links):
        decode = s * sub + (seat ^ i)
        prompt = decode - metas[n][:cap]
        here = (prompt >= 0) & (prompt < sub) & reaches(s, seat ^ i)
        wanted.append(jnp.where(here, prompt ^ seat, -1))
    infos = []
    for last in (False, True):
        rows_info = []
        for j in range(sub):
            length, table = metas[j][cap], metas[j][cap + 1 :]
            turn = (member - table // per_member) % members
            mine = (turn > 0) if last else (turn == 0)
            place = (turn - 1 if last else turn) * per_member + table % per_member
            live = jnp.clip(length - logical * BLOCK, 0, BLOCK)
            rank = jnp.sum((mine[None, :] & (logical[None, :] < logical[:, None])), axis=1)
            chosen = mine[:, None] & (rank[:, None] == logical[None, :])
            rows_info.append(jnp.sum(jnp.where(mine, live, 0))[None])
            rows_info.append(jnp.sum(jnp.where(chosen, place[:, None], 0), axis=0))
        infos.append(jnp.concatenate(rows_info + wanted).astype(jnp.int32))

    own_offset = offsets.reshape(-1).astype(jnp.int32)
    served = jnp.where(own_offset <= seat, 0, (own_offset - seat + sub - 1) // sub)
    seats = jnp.stack([seat ^ i for i in range(sub)])
    merge_info = jnp.concatenate([served, seats]).astype(jnp.int32)
    output = None
    near_chunks, far_chunks = [], []
    for chunks in stage_chunks:
        near_chunks.append([chunks[n] for n, (j, r) in enumerate(seats_of) if r == 0])
        far_chunks.append([chunks[n] for n, (j, r) in enumerate(seats_of) if r > 0])
    states = [
        prompt_call(
            sub, links, cap, group_size, blocks, infos[0], near_chunks[h], fetched[h], None
        )[0]
        for h in range(heads)
    ]
    states = lax.optimization_barrier(states)
    for h in range(heads):
        parts = prompt_call(
            sub, links, cap, group_size, blocks, infos[1], far_chunks[h], fetched[h], states[h]
        )
        results = []
        for n, (s, i) in enumerate(links):
            if s == 0 and i == 0:
                results.append(parts[n])
            else:
                results.append(lax.ppermute(parts[n], AXES, pairs_of(s, i, True)))
        output = merge_call(
            sub, heads, h, links, cap, group_size, merge_info, queries, new_cache, results, output
        )
    return output


def solution(mesh):
    in_specs = (
        P(None, ("group", "tensor"), None),
        P("group", None, "tensor"),
        P(None, "group", None, "tensor"),
        P("group", None),
        P("group"),
        P("group", None),
    )
    out_specs = P("group", None, "tensor")

    return jax.shard_map(shards, mesh=mesh, in_specs=in_specs, out_specs=out_specs, check_vma=False)
```
